1024 devices in a mesh: dp: 16 (over y, x), ctx: 64 (over z, core).
Axes of the slice: x: 4, y: 4, z: 32, core: 2. Of those that a mesh axis runs over, the one named last changes fastest.
Arguments:
- segment_ids: int32 [16, 8192], P('dp'), may hold values from 0 to 63, never falling along the last dimension, each value on 1 to 512 neighbouring positions
- queries: bfloat16 [16, 8192, 2048], P('dp', 'ctx'), may hold values from -600 to 600
- keys: bfloat16 [16, 8192, 1024], P('dp', 'ctx'), may hold values from -600 to 600
- values: bfloat16 [16, 8192, 1024], P('dp', 'ctx'), may hold values from -6 to 6
- query_gain: float32 [256], replicated, may hold values from 0.1 to 1.9
- key_gain: float32 [256], replicated, may hold values from 0.1 to 1.9
- out_grad: bfloat16 [16, 8192, 2048], P('dp', 'ctx'), may hold values from -9 to 9
Outputs:
- attended: bfloat16 [16, 8192, 2048], P('dp', 'ctx')
- query_grad: bfloat16 [16, 8192, 2048], P('dp', 'ctx')
- key_grad: bfloat16 [16, 8192, 1024], P('dp', 'ctx')
- value_grad: bfloat16 [16, 8192, 1024], P('dp', 'ctx')
- query_gain_grad: float32 [256], replicated
- key_gain_grad: float32 [256], replicated
The draws below stay inside these ranges and needn't reach their ends.
Inputs may be any that keep to these rules, and one draw needn't show every extreme that they name: `segment_ids`: in each packed sequence the document numbers never fall along the positions; every document holds 1 to 512 positions and one holds exactly 512.
All inputs are finite; a program needn't handle non-finite values.
Results may differ from the reference program's by a relative error of at most 0.0081.
Values may be sent and summed in bfloat16 or wider, within the bound.
A program may use at most 32 MiB of HBM per device.

```python
import math
import jax
import jax.numpy as jnp
import numpy as np
from jax import lax

HEADS = 8
KV_HEADS = 4
HEAD_DIM = 256
TOK_DEV = 128
GREACH = 4
SEQS = 16
SEQ_LEN = 8192
DOCS = 64
WINDOW = 512


def scaled_rows(key, heads):
    first = jax.random.fold_in(key, 0)
    second = jax.random.fold_in(key, 1)
    fourth = jax.random.fold_in(key, 3)
    shape = (SEQS, SEQ_LEN, heads, HEAD_DIM)
    base = jnp.clip(jax.random.normal(first, shape, jnp.float32), -6.0, 6.0)
    row_scale = 10.0 ** jax.random.uniform(second, (SEQS, SEQ_LEN, heads, 1), jnp.float32)
    col_scale = 10.0 ** jax.random.uniform(fourth, (HEAD_DIM,), jnp.float32)
    return (base * row_scale * col_scale).reshape(SEQS, SEQ_LEN, heads * HEAD_DIM)


def draw_queries(key, part):
    return scaled_rows(jax.random.fold_in(key, 101), HEADS).astype(jnp.bfloat16)


def draw_keys(key, part):
    return scaled_rows(jax.random.fold_in(key, 202), KV_HEADS).astype(jnp.bfloat16)


def draw_out_grad(key, part):
    inner = jax.random.fold_in(key, 303)
    shape = (SEQS, SEQ_LEN, HEADS * HEAD_DIM)
    along = jnp.arange(SEQ_LEN, dtype=jnp.float32) / SEQ_LEN
    across = jnp.arange(SEQS, dtype=jnp.float32) / SEQS
    rise = 0.25 * (1.0 + 2.0 * along)[None, :, None] * (1.0 + 2.0 * across)[:, None, None]
    base = jnp.clip(jax.random.normal(inner, shape, jnp.float32), -4.0, 4.0)
    return (base * rise).astype(jnp.bfloat16)


def block_scale(key, dims, cuts, low, high):
    factor_of = 1.0
    for dim, blocks in cuts:
        heights = jax.random.uniform(jax.random.fold_in(jax.random.fold_in(key, 6), dim), (blocks,), jnp.float32, low / len(cuts), high / len(cuts))
        factor_of = factor_of * jnp.repeat(jnp.exp(heights), dims[dim] // blocks).reshape((-1,) + (1,) * (len(dims) - 1 - dim))
    return factor_of


def profile(amount, total, most, lean):
    loads = [(1 << 20) // math.isqrt(standing ** lean) + 1 for standing in range(2, amount + 1)]
    spare, given = total - most - (amount - 1), [1] * (amount - 1)
    while spare > 0:
        candidates = [i for i in range(amount - 1) if given[i] < most]
        pool, remaining = sum([loads[i] for i in candidates]), spare
        for i in candidates:
            addition = min(most - given[i], max(1, remaining * loads[i] // pool), spare)
            given[i] = given[i] + addition
            spare = spare - addition
    return np.array([most] + given)


def uneven(rng, amount, total, most, skew):
    if amount == 2:
        one = jax.random.randint(rng, (), max(1, total - most), min(most, total - 1) + 1)
        return jnp.stack([one, total - one])
    lengths = jnp.asarray(profile(amount, total, most, skew), jnp.int32)
    twos = (amount - 1) // 2
    giver, receiver = lengths[1:1 + 2 * twos:2], lengths[2:2 + 2 * twos:2]
    slack = jnp.minimum(giver - 1, most - receiver)
    passed = jax.random.randint(jax.random.fold_in(rng, 1), (twos,), 0, 1 << 20) % (slack + 1)
    lengths = lengths.at[1:1 + 2 * twos:2].set(giver - passed).at[2:2 + 2 * twos:2].set(receiver + passed)
    return lengths[jax.random.permutation(jax.random.fold_in(rng, 2), amount)]


def noise(key, shape, spread, limit, cuts=(), kind=jnp.bfloat16):
    entries = jax.random.normal(key, shape, jnp.float32) * spread
    if len(cuts) > 0:
        entries = block_scale(key, shape, cuts, -0.22, 0.18) * entries
    return jnp.clip(entries, min=-limit, max=limit).astype(kind)


def setup_inputs(seed: int = 0) -> dict:
    arg_keys = jax.random.split(jax.random.key(seed), 8)
    segment_ids = jax.vmap(lambda own: jnp.searchsorted(jnp.cumsum(uneven(own, DOCS, SEQ_LEN, WINDOW, 2)), jnp.arange(SEQ_LEN), side="right"))(jax.random.split(arg_keys[0], SEQS)).reshape((SEQS, SEQ_LEN)).astype(jnp.int32)
    queries = draw_queries(jax.random.fold_in(arg_keys[7], 71), 0)
    keys = draw_keys(jax.random.fold_in(arg_keys[7], 71), 0)
    values = noise(arg_keys[3], (SEQS, SEQ_LEN, KV_HEADS * HEAD_DIM), 1.0, 6.0, ((0, 16), (1, 64)))
    query_gain = jnp.clip(1.0 + 0.18 * jax.random.normal(arg_keys[4], (HEAD_DIM,), jnp.float32), 0.1, 1.9)
    key_gain = jnp.clip(1.0 + 0.18 * jax.random.normal(arg_keys[5], (HEAD_DIM,), jnp.float32), 0.1, 1.9)
    out_grad = draw_out_grad(jax.random.fold_in(arg_keys[7], 71), 0)
    return dict(segment_ids=segment_ids, queries=queries, keys=keys, values=values, query_gain=query_gain, key_gain=key_gain, out_grad=out_grad)


epsilon = 1e-06

def normalize(field, gain_vec):
    as_float = field.astype(jnp.float32)
    inverse = lax.rsqrt(lax.optimization_barrier(jnp.mean(as_float * as_float, -1, keepdims=True)) + epsilon)
    normed = as_float * inverse
    return (normed, inverse, normed * gain_vec)

def norm_backward(upstream, normed, inverse, gain_vec):
    scaled = upstream * gain_vec
    grad_in = inverse * (scaled - normed * lax.optimization_barrier(jnp.mean(scaled * normed, -1, keepdims=True)))
    return (grad_in, lax.optimization_barrier(jnp.sum(upstream * normed, axis=(0, 1))))

def reference(segment_ids, queries, keys, values, query_gain, key_gain, out_grad):
    groups = HEADS // KV_HEADS
    reach_rows = GREACH * TOK_DEV
    blocks = SEQ_LEN // TOK_DEV
    band_rows = reach_rows + TOK_DEV
    column_ids = jnp.arange(band_rows)[None, :]
    row_ids = jnp.arange(TOK_DEV)[:, None]
    in_window = (column_ids <= row_ids + reach_rows) & (column_ids > row_ids)

    def banded(field):
        tiled = field.reshape((blocks + GREACH, TOK_DEV) + field.shape[1:])
        return jnp.concatenate([tiled[offset:offset + blocks] for offset in range(GREACH + 1)], axis=1)

    def folded(parts):
        pieces = parts.reshape(blocks, GREACH + 1, TOK_DEV, KV_HEADS, HEAD_DIM)
        summed = jnp.zeros((blocks + GREACH, TOK_DEV, KV_HEADS, HEAD_DIM), jnp.float32)
        for offset in range(GREACH + 1):
            summed = summed + jnp.pad(pieces[:, offset], ((offset, GREACH - offset), (0, 0), (0, 0), (0, 0)))
        return summed[GREACH:].reshape(SEQ_LEN, KV_HEADS, HEAD_DIM)

    def one_sequence(items):
        seg_row, query_seq, key_seq, value_seq, grad_seq = items
        q_normed, q_inverse, q_gained = normalize(query_seq.reshape(SEQ_LEN, HEADS, HEAD_DIM), query_gain)
        q_scaled = (q_gained * HEAD_DIM ** (-0.5)).astype(jnp.bfloat16)
        k_normed, k_inverse, k_gained = normalize(key_seq.reshape(SEQ_LEN, KV_HEADS, HEAD_DIM), key_gain)
        k_rounded = k_gained.astype(jnp.bfloat16)
        lead_zeros = jnp.zeros((reach_rows, KV_HEADS, HEAD_DIM), jnp.bfloat16)
        band_keys = banded(jnp.concatenate([lead_zeros, k_rounded])).astype(jnp.float32)
        band_values = banded(jnp.concatenate([lead_zeros, value_seq.reshape(SEQ_LEN, KV_HEADS, HEAD_DIM)])).astype(jnp.float32)
        band_seg = banded(jnp.concatenate([jnp.full((reach_rows,), -1, jnp.int32), seg_row.astype(jnp.int32)]))
        query_seg = seg_row.astype(jnp.int32).reshape(blocks, TOK_DEV)
        live_mask = (query_seg[:, :, None] == band_seg[:, None, :]) & in_window[None]
        q_grouped = q_scaled.astype(jnp.float32).reshape(blocks, TOK_DEV, KV_HEADS, groups, HEAD_DIM)
        scores = jnp.einsum('bikgd,bjkd->bkgij', q_grouped, band_keys)
        weights = jnp.where(live_mask[:, None, None], jnp.exp(scores), 0.0)
        probs = weights / lax.optimization_barrier(jnp.sum(weights, -1, keepdims=True))
        probs_back = lax.optimization_barrier(probs.astype(jnp.bfloat16)).astype(jnp.float32)
        attended = jnp.einsum('bkgij,bjkd->bikgd', probs_back, band_values)
        attended = attended.astype(jnp.bfloat16).reshape(SEQ_LEN, HEADS * HEAD_DIM)
        grad_grouped = grad_seq.astype(jnp.float32).reshape(blocks, TOK_DEV, KV_HEADS, groups, HEAD_DIM)
        dprob = jnp.einsum('bikgd,bjkd->bkgij', grad_grouped, band_values)
        centre = lax.optimization_barrier(jnp.sum(probs * dprob, -1, keepdims=True))
        dscore = lax.optimization_barrier((probs * (dprob - centre)).astype(jnp.bfloat16)).astype(jnp.float32)
        dq_scaled = jnp.einsum('bkgij,bjkd->bikgd', dscore, band_keys).reshape(SEQ_LEN, HEADS, HEAD_DIM)
        key_parts = jnp.einsum('bkgij,bikgd->bjkd', dscore, q_grouped)
        key_parts = lax.optimization_barrier(key_parts.astype(jnp.bfloat16)).astype(jnp.float32)
        value_parts = jnp.einsum('bkgij,bikgd->bjkd', probs_back, grad_grouped)
        value_parts = lax.optimization_barrier(value_parts.astype(jnp.bfloat16)).astype(jnp.float32)
        dk_rounded = folded(key_parts)
        value_grad = folded(value_parts).astype(jnp.bfloat16).reshape(SEQ_LEN, KV_HEADS * HEAD_DIM)
        query_grad, query_gain_part = norm_backward(dq_scaled * HEAD_DIM ** (-0.5), q_normed, q_inverse, query_gain)
        key_grad, key_gain_part = norm_backward(dk_rounded, k_normed, k_inverse, key_gain)
        return (attended, query_grad.astype(jnp.bfloat16).reshape(SEQ_LEN, HEADS * HEAD_DIM), key_grad.astype(jnp.bfloat16).reshape(SEQ_LEN, KV_HEADS * HEAD_DIM), value_grad, query_gain_part, key_gain_part)
    results = lax.map(one_sequence, (segment_ids, queries, keys, values, out_grad))
    factor = (SEQS * SEQ_LEN) ** (-0.5)
    return (results[0], results[1], results[2], results[3], lax.optimization_barrier(jnp.sum(results[4], 0)) * factor, lax.optimization_barrier(jnp.sum(results[5], 0)) * factor)
```

```python
import jax
import jax.numpy as jnp
from jax import lax
from jax.experimental import pallas as pl
from jax.experimental.pallas import tpu as pltpu
from jax.sharding import PartitionSpec as P

HEADS = 8
KV_HEADS = 4
GROUPS = HEADS // KV_HEADS
HEAD_DIM = 256
TOK = 128
GREACH = 4
BAND = GREACH + 1
ROWS = GROUPS * TOK
SIDE = 4
EPSILON = 1e-06
SCALE = HEAD_DIM ** (-0.5)

MESH = pl.DeviceIdType.MESH
F32 = jnp.float32
BF16 = jnp.bfloat16

NEXT, RELAY, NEAR, FAR = range(4)


def wrap(value, size):
    return lax.rem(value + size, size)


def dot_nt(a, b):
    return lax.dot_general(a, b, (((1,), (1,)), ((), ())), preferred_element_type=F32)


def dot_tn(a, b):
    return lax.dot_general(a, b, (((0,), (0,)), ((), ())), preferred_element_type=F32)


def dot_nn(a, b):
    return lax.dot_general(a, b, (((1,), (0,)), ((), ())), preferred_element_type=F32)


def inverse_norm(field):
    return lax.rsqrt(jnp.mean(field * field, -1, keepdims=True) + EPSILON)


def norm_backward(upstream, normed, inverse, gain):
    scaled = upstream * gain
    return inverse * (scaled - normed * jnp.mean(scaled * normed, -1, keepdims=True))


def head_columns(head):
    return pl.ds(head * HEAD_DIM, HEAD_DIM)


def kernel(
    ctx_size,
    factor,
    seg_hbm,
    q_hbm,
    k_hbm,
    v_hbm,
    q_gain,
    k_gain,
    g_hbm,
    att_out,
    dq_out,
    dk_out,
    dv_out,
    q_gain_out,
    k_gain_out,
    seg_rows,
    mask,
    q_raw,
    q_scaled,
    out_grad,
    k_raw,
    band,
    part_out,
    part_in,
    kept,
    sum_out,
    sum_in,
    gain_part,
    ar_x,
    ar_y,
    ar_z,
    ar_far,
    ar_core,
    load_sem,
    band_send,
    band_recv,
    part_send,
    part_recv,
    sum_send,
    sum_recv,
    ar_send,
    ar_recv,
    known,
):
    dp = lax.axis_index("dp")
    me = lax.axis_index("ctx")
    core = lax.rem(me, 2)
    z = lax.div(me, 2)
    x = lax.rem(dp, SIDE)
    y = lax.div(dp, SIDE)
    chips = ctx_size // 2

    partner = (dp, me + 1 - 2 * core)

    def along_z(step):
        return (dp, wrap(me + 2 * step, ctx_size))

    def along_x(step):
        return (y * SIDE + wrap(x + step, SIDE), me)

    def along_y(step):
        return (wrap(y + step, SIDE) * SIDE + x, me)

    ahead = along_z(1)
    behind = along_z(-1)

    loads = {}

    def load(name, slot, source, target):
        copy = pltpu.make_async_copy(source, target, load_sem.at[slot])
        copy.start()
        loads[name] = copy

    for head in range(KV_HEADS):
        load(("k", head), head, k_hbm.at[0, :, head_columns(head)], k_raw.at[head])
        load(("v", head), 4 + head, v_hbm.at[0, :, head_columns(head)], band.at[head, 0, 1])
    for distance in range(BAND):
        first = pl.multiple_of(jnp.maximum(me - distance, 0) * TOK, TOK)
        load(("s", distance), 24 + distance, seg_hbm.at[:, pl.ds(first, TOK)], seg_rows.at[distance])
    for head in range(HEADS):
        rows = pl.ds((head % GROUPS) * TOK, TOK)
        load(("q", head), 8 + head, q_hbm.at[0, :, head_columns(head)], q_raw.at[head])
        load(
            ("g", head),
            16 + head,
            g_hbm.at[0, :, head_columns(head)],
            out_grad.at[head // GROUPS, rows],
        )

    nearby = [along_z(1), along_z(-1), along_x(1), along_x(-1), along_y(1), along_y(-1)]
    barrier = pltpu.get_barrier_semaphore()
    for device in nearby + [partner]:
        pl.semaphore_signal(barrier, inc=1, device_id=device, device_id_type=MESH)

    def remote(source, target, send, recv, device):
        return pltpu.make_async_remote_copy(
            src_ref=source,
            dst_ref=target,
            send_sem=send,
            recv_sem=recv,
            device_id=device,
            device_id_type=MESH,
        )

    def band_copy(head, kind):
        source, target, device = {
            NEXT: (0, 2, ahead),
            RELAY: (2, 4, ahead),
            NEAR: (2 * core, 1, partner),
            FAR: (2 + 2 * core, 3, partner),
        }[kind]
        return remote(
            band.at[head, source],
            band.at[head, target],
            band_send.at[head, kind],
            band_recv.at[head, kind],
            device,
        )

    def part_copy(head):
        return remote(
            part_out.at[head], part_in.at[head], part_send.at[head], part_recv.at[head], partner
        )

    def sum_copy(head, stage):
        return remote(
            sum_out.at[head, stage],
            sum_in.at[head, stage],
            sum_send.at[head, stage],
            sum_recv.at[head, stage],
            behind,
        )

    def tell(stage, devices):
        for device in devices:
            pl.semaphore_signal(known.at[stage], inc=1, device_id=device, device_id_type=MESH)

    def hear(stage, count):
        pl.semaphore_wait(known.at[stage], count)

    def key_normed(head):
        field = k_raw[head].astype(F32)
        inverse = inverse_norm(field)
        return field * inverse, inverse

    def query_normed(head):
        field = q_raw[head].astype(F32)
        inverse = inverse_norm(field)
        return field * inverse, inverse

    def prepare_keys(head):
        loads["k", head].wait()
        normed, _ = key_normed(head)
        band[head, 0, 0] = (normed * k_gain[...]).astype(BF16)
        loads["v", head].wait()

    def prepare_queries(kv_head):
        for group in range(GROUPS):
            head = kv_head * GROUPS + group
            loads["q", head].wait()
            normed, _ = query_normed(head)
            q_scaled[kv_head, pl.ds(group * TOK, TOK)] = (normed * q_gain[...] * SCALE).astype(BF16)
            loads["g", head].wait()

    def prepare_mask():
        for distance in range(BAND):
            loads["s", distance].wait()
        query_seg = seg_rows[0].astype(F32)
        key_at = lax.broadcasted_iota(jnp.int32, (TOK, TOK), 0)
        query_at = lax.broadcasted_iota(jnp.int32, (TOK, TOK), 1)
        for distance in range(BAND):
            key_seg = jnp.where(me >= distance, seg_rows[distance].astype(F32), -1.0)
            key_column = jnp.broadcast_to(key_seg, (TOK, TOK)).T
            live = key_column == query_seg
            if distance == 0:
                live = live & (key_at <= query_at)
            if distance == GREACH:
                live = live & (key_at > query_at)
            weight = jnp.where(live, 1.0, 0.0)
            for group in range(GROUPS):
                mask[distance, :, pl.ds(group * TOK, TOK)] = weight

    def attend(head):
        queries = q_scaled[head]
        grads = out_grad[head]
        weights, dprobs = {}, {}
        total = jnp.zeros((1, ROWS), F32)
        weighted = jnp.zeros((1, ROWS), F32)
        for distance in range(BAND):
            weight = jnp.exp(dot_nt(band[head, distance, 0], queries)) * mask[distance]
            dprob = dot_nt(band[head, distance, 1], grads)
            total = total + jnp.sum(weight, 0, keepdims=True)
            weighted = weighted + jnp.sum(weight * dprob, 0, keepdims=True)
            weights[distance], dprobs[distance] = weight, dprob
        inverse = 1.0 / total
        centre = weighted * inverse
        attended = jnp.zeros((ROWS, HEAD_DIM), F32)
        dq_scaled = jnp.zeros((ROWS, HEAD_DIM), F32)
        for distance in (1, 3, 4, 2, 0):
            probs = weights[distance] * inverse
            dscore = (probs * (dprobs[distance] - centre)).astype(BF16)
            probs = probs.astype(BF16)
            key_part = dot_nn(dscore, queries)
            value_part = dot_nn(probs, grads)
            if distance % 2 == 1:
                part_out[head, distance // 2, 0] = key_part.astype(BF16)
                part_out[head, distance // 2, 1] = value_part.astype(BF16)
            else:
                kept[head, distance // 2, 0] = key_part
                kept[head, distance // 2, 1] = value_part
            attended = attended + dot_tn(probs, band[head, distance, 1])
            dq_scaled = dq_scaled + dot_tn(dscore, band[head, distance, 0])
            if distance == 4:
                part_copy(head).start()
        key_gain_part = jnp.sum(dq_scaled * queries.astype(F32), 0, keepdims=True)
        query_gain_part = jnp.zeros((1, HEAD_DIM), F32)
        for group in range(GROUPS):
            query_head = head * GROUPS + group
            rows = slice(group * TOK, (group + 1) * TOK)
            columns = head_columns(query_head)
            att_out[0, :, columns] = attended[rows].astype(BF16)
            normed, inverse_q = query_normed(query_head)
            upstream = dq_scaled[rows] * SCALE
            query_gain_part = query_gain_part + jnp.sum(upstream * normed, 0, keepdims=True)
            dq = norm_backward(upstream, normed, inverse_q, q_gain[...])
            dq_out[0, :, columns] = dq.astype(BF16)
        both = jnp.concatenate([query_gain_part, key_gain_part], axis=0)
        gain_part[...] = both if head == 0 else gain_part[...] + both

    def send_own(head):
        band_copy(head, NEXT).start()

    def pass_on(head):
        band_copy(head, NEXT).wait_recv()
        band_copy(head, RELAY).start()
        band_copy(head, NEAR).start()

    def share(head):
        band_copy(head, RELAY).wait_recv()
        band_copy(head, FAR).start()

    def band_ready(head):
        band_copy(head, NEAR).wait_recv()
        band_copy(head, FAR).wait_recv()

    def join_parts(head):
        part_copy(head).wait_recv()
        kept[head, core] = kept[head, core] + part_in[head, 0].astype(F32)
        kept[head, core + 1] = kept[head, core + 1] + part_in[head, 1].astype(F32)
        sum_out[head, 0] = kept[head, 2].astype(BF16)
        sum_copy(head, 0).start()

    def pass_back(head):
        sum_copy(head, 0).wait_recv()
        sum_out[head, 1] = (kept[head, 1] + sum_in[head, 0].astype(F32)).astype(BF16)
        sum_copy(head, 1).start()

    def finish_keys(head):
        sum_copy(head, 1).wait_recv()
        dk = kept[head, 0, 0] + sum_in[head, 1, 0].astype(F32)
        dv = kept[head, 0, 1] + sum_in[head, 1, 1].astype(F32)
        dv_out[0, :, head_columns(head)] = dv.astype(BF16)
        normed, inverse = key_normed(head)
        dk = norm_backward(dk, normed, inverse, k_gain[...])
        dk_out[0, :, head_columns(head)] = dk.astype(BF16)

    def ar_copies(stage, buffer, mine, size, device_of):
        sends, arrivals = [], []
        for step in range(1, size):
            other = wrap(mine + step, size)
            device = device_of(other)
            send = ar_send.at[stage, step]
            sends.append(remote(buffer.at[mine], buffer.at[mine], send, ar_recv.at[stage, mine], device))
            arrivals.append(remote(buffer.at[other], buffer.at[other], send, ar_recv.at[stage, other], device))
        return sends, arrivals

    def ar_start(stage, buffer, mine, size, device_of, value):
        buffer[mine] = value
        sends, arrivals = ar_copies(stage, buffer, mine, size, device_of)
        for copy in sends:
            copy.start()

        def finish():
            for copy in arrivals:
                copy.wait_recv()
            for copy in sends:
                copy.wait_send()
            total = buffer[0]
            for slot in range(1, size):
                total = total + buffer[slot]
            return total

        return finish

    quad = lax.div(z, SIDE)
    in_quad = lax.rem(z, SIDE)

    prepare_keys(0)
    pl.semaphore_wait(barrier, len(nearby) + 1)
    send_own(0)
    tell(0, nearby)
    prepare_keys(1)
    send_own(1)
    prepare_keys(2)
    prepare_keys(3)
    prepare_queries(0)
    hear(0, len(nearby))
    tell(1, [along_z(2), along_z(-2)])
    prepare_mask()
    pass_on(0)
    send_own(2)
    prepare_queries(1)
    hear(1, 2)
    tell(2, [along_z(4), along_z(-4)])
    pass_on(1)
    send_own(3)
    prepare_queries(2)
    prepare_queries(3)
    share(0)
    band_ready(0)
    attend(0)
    hear(2, 2)
    tell(3, [along_z(8), along_z(-8)])
    pass_on(2)
    join_parts(0)
    share(1)
    band_ready(1)
    attend(1)
    hear(3, 2)
    pass_on(3)
    join_parts(1)
    pass_back(0)
    share(2)
    band_ready(2)
    attend(2)
    join_parts(2)
    pass_back(1)
    finish_keys(0)
    share(3)
    band_ready(3)
    attend(3)

    finish = ar_start(0, ar_x, x, SIDE, lambda other: (y * SIDE + other, me), gain_part[...])
    join_parts(3)
    pass_back(2)
    finish = ar_start(1, ar_y, y, SIDE, lambda other: (other * SIDE + x, me), finish())
    finish_keys(1)
    finish = ar_start(
        2, ar_z, in_quad, SIDE, lambda other: (dp, (quad * SIDE + other) * 2 + core), finish()
    )
    pass_back(3)
    finish = ar_start(
        3,
        ar_far,
        quad,
        chips // SIDE,
        lambda other: (dp, (other * SIDE + in_quad) * 2 + core),
        finish(),
    )
    finish_keys(2)
    finish_keys(3)
    finish = ar_start(4, ar_core, core, 2, lambda other: partner, finish())
    total = finish() * factor
    q_gain_out[...] = total[0:1]
    k_gain_out[...] = total[1:2] / k_gain[...]

    for head in range(KV_HEADS):
        for kind in range(4):
            band_copy(head, kind).wait_send()
        part_copy(head).wait_send()
        for stage in range(2):
            sum_copy(head, stage).wait_send()


def shards(segment_ids, queries, keys, values, query_gain, key_gain, out_grad):
    ctx_size = lax.axis_size("ctx")
    factor = (lax.axis_size("dp") * queries.shape[0] * ctx_size * queries.shape[1]) ** (-0.5)
    width = KV_HEADS * HEAD_DIM
    hbm = pl.BlockSpec(memory_space=pltpu.HBM)
    vmem = pl.BlockSpec(memory_space=pltpu.VMEM)
    dma = pltpu.SemaphoreType.DMA
    pair = (2, TOK, HEAD_DIM)
    quads = ctx_size // 2 // SIDE
    outs = pl.pallas_call(
        lambda *refs: kernel(ctx_size, factor, *refs),
        out_shape=(
            jax.ShapeDtypeStruct((1, TOK, HEADS * HEAD_DIM), BF16),
            jax.ShapeDtypeStruct((1, TOK, HEADS * HEAD_DIM), BF16),
            jax.ShapeDtypeStruct((1, TOK, width), BF16),
            jax.ShapeDtypeStruct((1, TOK, width), BF16),
            jax.ShapeDtypeStruct((1, HEAD_DIM), F32),
            jax.ShapeDtypeStruct((1, HEAD_DIM), F32),
        ),
        in_specs=[hbm, hbm, hbm, hbm, vmem, vmem, hbm],
        out_specs=(vmem,) * 6,
        scratch_shapes=[
            pltpu.VMEM((BAND, 1, TOK), jnp.int32),
            pltpu.VMEM((BAND, TOK, ROWS), F32),
            pltpu.VMEM((HEADS, TOK, HEAD_DIM), BF16),
            pltpu.VMEM((KV_HEADS, ROWS, HEAD_DIM), BF16),
            pltpu.VMEM((KV_HEADS, ROWS, HEAD_DIM), BF16),
            pltpu.VMEM((KV_HEADS, TOK, HEAD_DIM), BF16),
            pltpu.VMEM((KV_HEADS, BAND) + pair, BF16),
            pltpu.VMEM((KV_HEADS, 2) + pair, BF16),
            pltpu.VMEM((KV_HEADS, 2) + pair, BF16),
            pltpu.VMEM((KV_HEADS, 3) + pair, F32),
            pltpu.VMEM((KV_HEADS, 2) + pair, BF16),
            pltpu.VMEM((KV_HEADS, 2) + pair, BF16),
            pltpu.VMEM((2, HEAD_DIM), F32),
            pltpu.VMEM((SIDE, 2, HEAD_DIM), F32),
            pltpu.VMEM((SIDE, 2, HEAD_DIM), F32),
            pltpu.VMEM((SIDE, 2, HEAD_DIM), F32),
            pltpu.VMEM((quads, 2, HEAD_DIM), F32),
            pltpu.VMEM((2, 2, HEAD_DIM), F32),
            dma((24 + BAND,)),
            dma((KV_HEADS, 4)),
            dma((KV_HEADS, 4)),
            dma((KV_HEADS,)),
            dma((KV_HEADS,)),
            dma((KV_HEADS, 2)),
            dma((KV_HEADS, 2)),
            dma((5, quads)),
            dma((5, quads)),
            pltpu.SemaphoreType.REGULAR((4,)),
        ],
        compiler_params=pltpu.CompilerParams(
            collective_id=0, has_side_effects=True, vmem_limit_bytes=67043328
        ),
    )(
        segment_ids,
        queries,
        keys,
        values,
        query_gain.reshape(1, HEAD_DIM),
        key_gain.reshape(1, HEAD_DIM),
        out_grad,
    )
    return (*outs[:4], outs[4].reshape(HEAD_DIM), outs[5].reshape(HEAD_DIM))


def solution(mesh):
    blocks = P("dp", "ctx", None)
    return jax.shard_map(
        shards,
        mesh=mesh,
        in_specs=(P("dp", None), blocks, blocks, blocks, P(), P(), blocks),
        out_specs=(blocks, blocks, blocks, blocks, P(), P()),
        check_vma=False,
    )
```

```python
import jax
import jax.numpy as jnp
from jax import lax
from jax.experimental import pallas as pl
from jax.experimental.pallas import tpu as pltpu
from jax.sharding import PartitionSpec as P

HEADS = 8
KV_HEADS = 4
GROUPS = HEADS // KV_HEADS
HEAD_DIM = 256
TOK = 128
GREACH = 4
BAND = GREACH + 1
ROWS = GROUPS * TOK
SIDE = 4
EPSILON = 1e-06
SCALE = HEAD_DIM ** (-0.5)

MESH = pl.DeviceIdType.MESH
F32 = jnp.float32
BF16 = jnp.bfloat16

NEXT, RELAY, NEAR, FAR, FIRST = range(5)


def wrap(value, size):
    return lax.rem(value + size, size)


def dot_nt(a, b):
    return lax.dot_general(a, b, (((1,), (1,)), ((), ())), preferred_element_type=F32)


def dot_tn(a, b):
    return lax.dot_general(a, b, (((0,), (0,)), ((), ())), preferred_element_type=F32)


def dot_nn(a, b):
    return lax.dot_general(a, b, (((1,), (0,)), ((), ())), preferred_element_type=F32)


def inverse_norm(field):
    return lax.rsqrt(jnp.mean(field * field, -1, keepdims=True) + EPSILON)


def norm_backward(upstream, normed, inverse, gain):
    scaled = upstream * gain
    return inverse * (scaled - normed * jnp.mean(scaled * normed, -1, keepdims=True))


def head_columns(head):
    return pl.ds(head * HEAD_DIM, HEAD_DIM)


def kernel(
    ctx_size,
    factor,
    seg_hbm,
    q_hbm,
    k_hbm,
    v_hbm,
    q_gain_hbm,
    k_gain_hbm,
    g_hbm,
    att_hbm,
    dq_hbm,
    dk_hbm,
    dv_hbm,
    q_gain_grad_hbm,
    k_gain_grad_hbm,
    q_gain,
    k_gain,
    seg_rows,
    mask,
    q_raw,
    q_scaled,
    out_grad,
    k_raw,
    band,
    part_out,
    part_in,
    kept,
    sum_out,
    sum_in,
    att_buf,
    dq_buf,
    dk_buf,
    dv_buf,
    gain_part,
    gain_grads,
    ar_plane,
    ar_z,
    ar_core,
    load_sem,
    store_sem,
    band_send,
    band_recv,
    part_send,
    part_recv,
    sum_send,
    sum_recv,
    ar_send,
    ar_recv,
    known,
):
    dp = lax.axis_index("dp")
    me = lax.axis_index("ctx")
    core = lax.rem(me, 2)
    z = lax.div(me, 2)
    x = lax.rem(dp, SIDE)
    y = lax.div(dp, SIDE)
    chips = ctx_size // 2

    partner = (dp, me + 1 - 2 * core)

    def along_z(step):
        return (dp, wrap(me + 2 * step, ctx_size))

    def along_x(step):
        return (y * SIDE + wrap(x + step, SIDE), me)

    def along_y(step):
        return (wrap(y + step, SIDE) * SIDE + x, me)

    ahead = along_z(1)
    behind = along_z(-1)

    nearby = [along_z(1), along_z(-1), along_x(1), along_x(-1), along_y(1), along_y(-1)]
    barrier = pltpu.get_barrier_semaphore()
    for device in nearby + [partner]:
        pl.semaphore_signal(barrier, inc=1, device_id=device, device_id_type=MESH)

    loads = {}

    def load(name, slot, source, target):
        copy = pltpu.make_async_copy(source, target, load_sem.at[slot])
        copy.start()
        loads[name] = copy

    load("k_gain", 24 + BAND, k_gain_hbm, k_gain)
    load("q_gain", 25 + BAND, q_gain_hbm, q_gain)
    for head in range(KV_HEADS):
        load(("k", head), head, k_hbm.at[0, :, head_columns(head)], k_raw.at[head])
        load(("v", head), 4 + head, v_hbm.at[0, :, head_columns(head)], band.at[head, 0, 1])
    for distance in range(BAND):
        first = pl.multiple_of(jnp.maximum(me - distance, 0) * TOK, TOK)
        load(("s", distance), 24 + distance, seg_hbm.at[:, pl.ds(first, TOK)], seg_rows.at[distance])
    for head in range(HEADS):
        rows = pl.ds((head % GROUPS) * TOK, TOK)
        load(("q", head), 8 + head, q_hbm.at[0, :, head_columns(head)], q_raw.at[head])
        load(
            ("g", head),
            16 + head,
            g_hbm.at[0, :, head_columns(head)],
            out_grad.at[head // GROUPS, rows],
        )

    def remote(source, target, send, recv, device):
        return pltpu.make_async_remote_copy(
            src_ref=source,
            dst_ref=target,
            send_sem=send,
            recv_sem=recv,
            device_id=device,
            device_id_type=MESH,
        )

    def band_copy(head, kind):
        slot, target, device = {
            NEXT: (0, 2, ahead),
            RELAY: (2, 4, ahead),
            NEAR: (2 * core, 1, partner),
            FAR: (2 + 2 * core, 3, partner),
            FIRST: (0, 2, ahead),
        }[kind]
        source, target = band.at[head, slot], band.at[head, target]
        if kind == FIRST:
            source, target = v_hbm.at[0, :, head_columns(head)], band.at[head, 2, 1]
        elif kind == NEXT and head == 0:
            source, target = band.at[head, 0, 0], band.at[head, 2, 0]
        return remote(
            source,
            target,
            band_send.at[head, kind],
            band_recv.at[head, kind],
            device,
        )

    def part_copy(head):
        return remote(
            part_out.at[head], part_in.at[head], part_send.at[head], part_recv.at[head], partner
        )

    def sum_copy(head, stage):
        return remote(
            sum_out.at[head, stage],
            sum_in.at[head, stage],
            sum_send.at[head, stage],
            sum_recv.at[head, stage],
            behind,
        )

    def tell(stage, devices):
        for device in devices:
            pl.semaphore_signal(known.at[stage], inc=1, device_id=device, device_id_type=MESH)

    def hear(stage, count):
        pl.semaphore_wait(known.at[stage], count)

    def key_normed(head):
        field = k_raw[head].astype(F32)
        inverse = inverse_norm(field)
        return field * inverse, inverse

    def query_normed(head):
        field = q_raw[head].astype(F32)
        inverse = inverse_norm(field)
        return field * inverse, inverse

    def prepare_keys(head):
        loads["k", head].wait()
        normed, _ = key_normed(head)
        band[head, 0, 0] = (normed * k_gain[...]).astype(BF16)
        loads["v", head].wait()

    def prepare_queries(kv_head):
        for group in range(GROUPS):
            head = kv_head * GROUPS + group
            loads["q", head].wait()
            normed, _ = query_normed(head)
            q_scaled[kv_head, pl.ds(group * TOK, TOK)] = (normed * q_gain[...] * SCALE).astype(BF16)
            loads["g", head].wait()

    def prepare_mask():
        for distance in range(BAND):
            loads["s", distance].wait()
        query_seg = seg_rows[0].astype(F32)
        key_at = lax.broadcasted_iota(jnp.int32, (TOK, TOK), 0)
        query_at = lax.broadcasted_iota(jnp.int32, (TOK, TOK), 1)
        for distance in range(BAND):
            key_seg = jnp.where(me >= distance, seg_rows[distance].astype(F32), -1.0)
            key_column = jnp.broadcast_to(key_seg, (TOK, TOK)).T
            live = key_column == query_seg
            if distance == 0:
                live = live & (key_at <= query_at)
            if distance == GREACH:
                live = live & (key_at > query_at)
            weight = jnp.where(live, 1.0, 0.0)
            for group in range(GROUPS):
                mask[distance, :, pl.ds(group * TOK, TOK)] = weight

    stores = []

    def store(slot, source, target):
        copy = pltpu.make_async_copy(source, target, store_sem.at[slot])
        copy.start()
        stores.append(copy)

    def score(head, distances, state):
        total, weighted, weights, dprobs = state
        queries = q_scaled[head]
        grads = out_grad[head]
        for distance in distances:
            weight = jnp.exp(dot_nt(band[head, distance, 0], queries)) * mask[distance]
            dprob = dot_nt(band[head, distance, 1], grads)
            total = total + jnp.sum(weight, 0, keepdims=True)
            weighted = weighted + jnp.sum(weight * dprob, 0, keepdims=True)
            weights = weights | {distance: weight}
            dprobs = dprobs | {distance: dprob}
        return total, weighted, weights, dprobs

    def begin(head):
        band_copy(head, NEAR).wait_recv()
        zero = jnp.zeros((1, ROWS), F32)
        return score(head, (0, 2, 1), (zero, zero, {}, {}))

    def attend(head, state, after_gains=None):
        band_copy(head, FAR).wait_recv()
        total, weighted, weights, dprobs = score(head, (4, 3), state)
        queries = q_scaled[head]
        grads = out_grad[head]
        inverse = 1.0 / total
        centre = weighted * inverse
        probs, dscores = {}, {}
        dq_scaled = jnp.zeros((ROWS, HEAD_DIM), F32)
        for distance in range(BAND):
            prob = weights[distance] * inverse
            dscores[distance] = (prob * (dprobs[distance] - centre)).astype(BF16)
            probs[distance] = prob.astype(BF16)
            dq_scaled = dq_scaled + dot_tn(dscores[distance], band[head, distance, 0])
        key_gain_part = jnp.sum(dq_scaled * queries.astype(F32), 0, keepdims=True)
        query_gain_part = jnp.zeros((1, HEAD_DIM), F32)
        for group in range(GROUPS):
            normed, _ = query_normed(head * GROUPS + group)
            upstream = dq_scaled[group * TOK : (group + 1) * TOK] * SCALE
            query_gain_part = query_gain_part + jnp.sum(upstream * normed, 0, keepdims=True)
        both = jnp.concatenate([query_gain_part, key_gain_part], axis=0)
        gain_part[...] = both if head == 0 else gain_part[...] + both
        later = after_gains() if after_gains else None
        for distance in (1, 3):
            key_part = dot_nn(dscores[distance], queries)
            value_part = dot_nn(probs[distance], grads)
            part_out[head, distance // 2, 0] = key_part.astype(BF16)
            part_out[head, distance // 2, 1] = value_part.astype(BF16)
        attended = jnp.zeros((ROWS, HEAD_DIM), F32)
        for distance in (4, 2, 0):
            kept[head, distance // 2, 0] = dot_nn(dscores[distance], queries)
            kept[head, distance // 2, 1] = dot_nn(probs[distance], grads)
            if distance == 4:
                part_copy(head).start()
        for distance in range(BAND):
            attended = attended + dot_tn(probs[distance], band[head, distance, 1])
        for group in range(GROUPS):
            query_head = head * GROUPS + group
            rows = slice(group * TOK, (group + 1) * TOK)
            att_buf[query_head] = attended[rows].astype(BF16)
            normed, inverse_q = query_normed(query_head)
            dq = norm_backward(dq_scaled[rows] * SCALE, normed, inverse_q, q_gain[...])
            dq_buf[query_head] = dq.astype(BF16)
            store(16 + query_head, att_buf.at[query_head], att_hbm.at[0, :, head_columns(query_head)])
            store(8 + query_head, dq_buf.at[query_head], dq_hbm.at[0, :, head_columns(query_head)])
        return later

    def send_own(head):
        band_copy(head, NEXT).start()

    def pass_on(head):
        band_copy(head, NEXT).wait_recv()
        if head == 0:
            band_copy(head, FIRST).wait_recv()
        band_copy(head, RELAY).start()
        band_copy(head, NEAR).start()

    def share(head):
        band_copy(head, RELAY).wait_recv()
        band_copy(head, FAR).start()

    def join_parts(head):
        part_copy(head).wait_recv()
        kept[head, core] = kept[head, core] + part_in[head, 0].astype(F32)
        kept[head, core + 1] = kept[head, core + 1] + part_in[head, 1].astype(F32)
        sum_out[head, 0] = kept[head, 2].astype(BF16)
        sum_copy(head, 0).start()

    def pass_back(head):
        sum_copy(head, 0).wait_recv()
        sum_out[head, 1] = (kept[head, 1] + sum_in[head, 0].astype(F32)).astype(BF16)
        sum_copy(head, 1).start()

    def finish_keys(head):
        sum_copy(head, 1).wait_recv()
        dk = kept[head, 0, 0] + sum_in[head, 1, 0].astype(F32)
        dv = kept[head, 0, 1] + sum_in[head, 1, 1].astype(F32)
        dv_buf[head] = dv.astype(BF16)
        normed, inverse = key_normed(head)
        dk = norm_backward(dk, normed, inverse, k_gain[...])
        dk_buf[head] = dk.astype(BF16)
        store(4 + head, dv_buf.at[head], dv_hbm.at[0, :, head_columns(head)])
        store(head, dk_buf.at[head], dk_hbm.at[0, :, head_columns(head)])

    def ar_start(stage, buffer, mine, size, device_of, value):
        buffer[mine] = value
        sends, arrivals = [], []
        steps = sorted(range(1, size), key=lambda step: -min(step, size - step))
        for step in steps:
            other = wrap(mine + step, size)
            send = ar_send.at[stage, step]
            sends.append(
                remote(buffer.at[mine], buffer.at[mine], send, ar_recv.at[stage, mine], device_of(other))
            )
            arrivals.append(
                remote(
                    buffer.at[other], buffer.at[other], send, ar_recv.at[stage, other], device_of(other)
                )
            )
        for copy in sends:
            copy.start()

        def finish():
            for copy in arrivals:
                copy.wait_recv()
            for copy in sends:
                copy.wait_send()
            total = buffer[0]
            for slot in range(1, size):
                total = total + buffer[slot]
            return total

        return finish

    pl.semaphore_wait(barrier, len(nearby) + 1)
    band_copy(0, FIRST).start()
    loads["k_gain"].wait()
    prepare_keys(0)
    send_own(0)
    tell(0, nearby)
    prepare_keys(1)
    send_own(1)
    prepare_keys(2)
    prepare_keys(3)
    loads["q_gain"].wait()
    prepare_queries(0)
    hear(0, len(nearby))
    tell(1, [along_z(2), along_z(-2), along_x(2), along_y(2)])
    prepare_mask()
    pass_on(0)
    send_own(2)
    prepare_queries(1)
    hear(1, 4)
    tell(2, [along_z(4), along_z(-4)])
    pass_on(1)
    send_own(3)
    prepare_queries(2)
    prepare_queries(3)
    state = begin(0)
    share(0)
    attend(0, state)
    pass_on(2)
    hear(2, 2)
    tell(3, [along_z(8), along_z(-8)])
    join_parts(0)
    state = begin(1)
    share(1)
    attend(1, state)
    pass_on(3)
    join_parts(1)
    pass_back(0)
    state = begin(2)
    share(2)
    attend(2, state)
    hear(3, 2)
    share(3)
    join_parts(2)
    pass_back(1)
    state = begin(3)
    finish = attend(
        3,
        state,
        lambda: ar_start(0, ar_plane, dp, SIDE * SIDE, lambda other: (other, me), gain_part[...]),
    )
    finish_keys(0)
    join_parts(3)
    finish = ar_start(1, ar_z, z, chips, lambda other: (dp, other * 2 + core), finish())
    pass_back(2)
    finish_keys(1)
    pass_back(3)
    finish_keys(2)
    finish_keys(3)
    finish = ar_start(2, ar_core, core, 2, lambda other: partner, finish())
    total = finish() * factor
    gain_grads[0] = total[0:1]
    gain_grads[1] = total[1:2] / k_gain[...]
    store(24, gain_grads.at[0], q_gain_grad_hbm)
    store(25, gain_grads.at[1], k_gain_grad_hbm)

    for head in range(KV_HEADS):
        for kind in range(4):
            band_copy(head, kind).wait_send()
        part_copy(head).wait_send()
        for stage in range(2):
            sum_copy(head, stage).wait_send()
    band_copy(0, FIRST).wait_send()
    for copy in stores:
        copy.wait()


def hand_over(count, *refs):
    sources, targets = refs[:count], refs[count : 2 * count]
    buffers, semaphores = refs[2 * count : 3 * count], refs[3 * count]
    loads = [
        pltpu.make_async_copy(source, buffer, semaphores.at[0, slot])
        for slot, (source, buffer) in enumerate(zip(sources, buffers))
    ]
    stores = [
        pltpu.make_async_copy(buffer, target, semaphores.at[1, slot])
        for slot, (buffer, target) in enumerate(zip(buffers, targets))
    ]
    for load in loads:
        load.start()
    for load, store in zip(loads, stores):
        load.wait()
        store.start()
    for store in stores:
        store.wait()


def shards(segment_ids, queries, keys, values, query_gain, key_gain, out_grad):
    ctx_size = lax.axis_size("ctx")
    factor = (lax.axis_size("dp") * queries.shape[0] * ctx_size * queries.shape[1]) ** (-0.5)
    width = KV_HEADS * HEAD_DIM
    hbm = pl.BlockSpec(memory_space=pl.ANY)
    dma = pltpu.SemaphoreType.DMA
    pair = (2, TOK, HEAD_DIM)
    chips = ctx_size // 2
    shapes = (
        jax.ShapeDtypeStruct((1, TOK, HEADS * HEAD_DIM), BF16),
        jax.ShapeDtypeStruct((1, TOK, HEADS * HEAD_DIM), BF16),
        jax.ShapeDtypeStruct((1, TOK, width), BF16),
        jax.ShapeDtypeStruct((1, TOK, width), BF16),
        jax.ShapeDtypeStruct((1, HEAD_DIM), F32),
        jax.ShapeDtypeStruct((1, HEAD_DIM), F32),
    )
    outs = pl.pallas_call(
        lambda *refs: kernel(ctx_size, factor, *refs),
        out_shape=shapes,
        in_specs=[hbm] * 7,
        out_specs=(hbm,) * len(shapes),
        scratch_shapes=[
            pltpu.VMEM((1, HEAD_DIM), F32),
            pltpu.VMEM((1, HEAD_DIM), F32),
            pltpu.VMEM((BAND, 1, TOK), jnp.int32),
            pltpu.VMEM((BAND, TOK, ROWS), F32),
            pltpu.VMEM((HEADS, TOK, HEAD_DIM), BF16),
            pltpu.VMEM((KV_HEADS, ROWS, HEAD_DIM), BF16),
            pltpu.VMEM((KV_HEADS, ROWS, HEAD_DIM), BF16),
            pltpu.VMEM((KV_HEADS, TOK, HEAD_DIM), BF16),
            pltpu.VMEM((KV_HEADS, BAND) + pair, BF16),
            pltpu.VMEM((KV_HEADS, 2) + pair, BF16),
            pltpu.VMEM((KV_HEADS, 2) + pair, BF16),
            pltpu.VMEM((KV_HEADS, 3) + pair, F32),
            pltpu.VMEM((KV_HEADS, 2) + pair, BF16),
            pltpu.VMEM((KV_HEADS, 2) + pair, BF16),
            pltpu.VMEM((HEADS, TOK, HEAD_DIM), BF16),
            pltpu.VMEM((HEADS, TOK, HEAD_DIM), BF16),
            pltpu.VMEM((KV_HEADS, TOK, HEAD_DIM), BF16),
            pltpu.VMEM((KV_HEADS, TOK, HEAD_DIM), BF16),
            pltpu.VMEM((2, HEAD_DIM), F32),
            pltpu.VMEM((2, 1, HEAD_DIM), F32),
            pltpu.VMEM((SIDE * SIDE, 2, HEAD_DIM), F32),
            pltpu.VMEM((chips, 2, HEAD_DIM), F32),
            pltpu.VMEM((2, 2, HEAD_DIM), F32),
            dma((26 + BAND,)),
            dma((26,)),
            dma((KV_HEADS, 5)),
            dma((KV_HEADS, 5)),
            dma((KV_HEADS,)),
            dma((KV_HEADS,)),
            dma((KV_HEADS, 2)),
            dma((KV_HEADS, 2)),
            dma((3, chips)),
            dma((3, chips)),
            pltpu.SemaphoreType.REGULAR((4,)),
        ],
        compiler_params=pltpu.CompilerParams(
            collective_id=0, has_side_effects=True, vmem_limit_bytes=67043328
        ),
    )(
        segment_ids,
        queries,
        keys,
        values,
        query_gain.reshape(1, HEAD_DIM),
        key_gain.reshape(1, HEAD_DIM),
        out_grad,
    )
    outs = pl.pallas_call(
        lambda *refs: hand_over(len(shapes), *refs),
        out_shape=shapes,
        in_specs=[hbm] * len(shapes),
        out_specs=(hbm,) * len(shapes),
        scratch_shapes=[pltpu.VMEM(shape.shape, shape.dtype) for shape in shapes]
        + [dma((2, len(shapes)))],
        compiler_params=pltpu.CompilerParams(vmem_limit_bytes=67043328),
    )(*outs)
    return (*outs[:4], outs[4].reshape(HEAD_DIM), outs[5].reshape(HEAD_DIM))


def solution(mesh):
    blocks = P("dp", "ctx", None)
    return jax.shard_map(
        shards,
        mesh=mesh,
        in_specs=(P("dp", None), blocks, blocks, blocks, P(), P(), blocks),
        out_specs=(blocks, blocks, blocks, blocks, P(), P()),
        check_vma=False,
    )
```

```python
import jax
import jax.numpy as jnp
from jax import lax
from jax.experimental import pallas as pl
from jax.experimental.pallas import tpu as pltpu
from jax.sharding import PartitionSpec as P

HEADS = 8
KV_HEADS = 4
GROUPS = HEADS // KV_HEADS
HEAD_DIM = 256
TOK = 128
GREACH = 4
BAND = GREACH + 1
ROWS = GROUPS * TOK
SIDE = 4
EPSILON = 1e-06
SCALE = HEAD_DIM ** (-0.5)

MESH = pl.DeviceIdType.MESH
F32 = jnp.float32
BF16 = jnp.bfloat16

NEXT, RELAY, NEAR, FAR, FIRST = range(5)


def wrap(value, size):
    return lax.rem(value + size, size)


def dot_nt(a, b):
    return lax.dot_general(a, b, (((1,), (1,)), ((), ())), preferred_element_type=F32)


def dot_tn(a, b):
    return lax.dot_general(a, b, (((0,), (0,)), ((), ())), preferred_element_type=F32)


def dot_nn(a, b):
    return lax.dot_general(a, b, (((1,), (0,)), ((), ())), preferred_element_type=F32)


def inverse_norm(field):
    return lax.rsqrt(jnp.mean(field * field, -1, keepdims=True) + EPSILON)


def norm_backward(upstream, normed, inverse, gain):
    scaled = upstream * gain
    return inverse * (scaled - normed * jnp.mean(scaled * normed, -1, keepdims=True))


def head_columns(head):
    return pl.ds(head * HEAD_DIM, HEAD_DIM)


def kernel(
    ctx_size,
    factor,
    seg_hbm,
    q_hbm,
    k_hbm,
    v_hbm,
    q_gain_hbm,
    k_gain_hbm,
    g_hbm,
    att_hbm,
    dq_hbm,
    dk_hbm,
    dv_hbm,
    q_gain_grad_hbm,
    k_gain_grad_hbm,
    q_gain,
    k_gain,
    seg_rows,
    mask,
    q_raw,
    q_scaled,
    g_raw,
    k_raw,
    band,
    part_out,
    part_in,
    kept,
    sum_out,
    sum_in,
    att_buf,
    dq_buf,
    dk_buf,
    dv_buf,
    gain_part,
    gain_rows,
    gain_grads,
    ar_plane,
    ar_z,
    ar_core,
    load_sem,
    store_sem,
    band_send,
    band_recv,
    part_send,
    part_recv,
    sum_send,
    sum_recv,
    ar_send,
    ar_recv,
    known,
):
    dp = lax.axis_index("dp")
    me = lax.axis_index("ctx")
    core = lax.rem(me, 2)
    z = lax.div(me, 2)
    x = lax.rem(dp, SIDE)
    y = lax.div(dp, SIDE)
    chips = ctx_size // 2

    partner = (dp, me + 1 - 2 * core)

    def along_z(step):
        return (dp, wrap(me + 2 * step, ctx_size))

    def along_x(step):
        return (y * SIDE + wrap(x + step, SIDE), me)

    def along_y(step):
        return (wrap(y + step, SIDE) * SIDE + x, me)

    ahead = along_z(1)
    behind = along_z(-1)

    nearby = [along_z(1), along_z(-1), along_x(1), along_x(-1), along_y(1), along_y(-1)]
    barrier = pltpu.get_barrier_semaphore()
    for device in nearby + [partner]:
        pl.semaphore_signal(barrier, inc=1, device_id=device, device_id_type=MESH)

    loads = {}

    def load(name, slot, source, target):
        copy = pltpu.make_async_copy(source, target, load_sem.at[slot])
        copy.start()
        loads[name] = copy

    rest = pl.ds(HEAD_DIM, (KV_HEADS - 1) * HEAD_DIM)
    load("k_gain", 0, k_gain_hbm, k_gain)
    load(("k", 0), 1, k_hbm.at[0, :, head_columns(0)], k_raw.at[:, head_columns(0)])
    load(("v", 0), 2, v_hbm.at[0, :, head_columns(0)], band.at[0, 0, 1])
    load(("k", 1), 3, k_hbm.at[0, :, rest], k_raw.at[:, rest])
    for head in range(1, KV_HEADS):
        load(("v", head), 3 + head, v_hbm.at[0, :, head_columns(head)], band.at[head, 0, 1])
    load("q_gain", 7, q_gain_hbm, q_gain)
    load("q", 8, q_hbm.at[0], q_raw)
    load("g", 9, g_hbm.at[0], g_raw)
    for distance in range(BAND):
        first = pl.multiple_of(jnp.maximum(me - distance, 0) * TOK, TOK)
        load(("s", distance), 10 + distance, seg_hbm.at[:, pl.ds(first, TOK)], seg_rows.at[distance])

    def remote(source, target, send, recv, device):
        return pltpu.make_async_remote_copy(
            src_ref=source,
            dst_ref=target,
            send_sem=send,
            recv_sem=recv,
            device_id=device,
            device_id_type=MESH,
        )

    def band_copy(head, kind):
        slot, target, device = {
            NEXT: (0, 2, ahead),
            RELAY: (2, 4, ahead),
            NEAR: (2 * core, 1, partner),
            FAR: (2 + 2 * core, 3, partner),
            FIRST: (0, 2, ahead),
        }[kind]
        source, target = band.at[head, slot], band.at[head, target]
        if kind == FIRST:
            source, target = v_hbm.at[0, :, head_columns(head)], band.at[head, 2, 1]
        elif kind == NEXT and head == 0:
            source, target = band.at[head, 0, 0], band.at[head, 2, 0]
        return remote(
            source,
            target,
            band_send,
            band_recv.at[head, kind],
            device,
        )

    def part_copy(head):
        return remote(
            part_out.at[head], part_in.at[head], part_send, part_recv.at[head], partner
        )

    def sum_copy(head, stage):
        return remote(
            sum_out.at[head, stage],
            sum_in.at[head, stage],
            sum_send,
            sum_recv.at[head, stage],
            behind,
        )

    def tell(stage, devices):
        for device in devices:
            pl.semaphore_signal(known.at[stage], inc=1, device_id=device, device_id_type=MESH)

    def hear(stage, count):
        pl.semaphore_wait(known.at[stage], count)

    def key_normed(head):
        field = k_raw[:, head_columns(head)].astype(F32)
        inverse = inverse_norm(field)
        return field * inverse, inverse

    def query_normed(head):
        field = q_raw[:, head_columns(head)].astype(F32)
        inverse = inverse_norm(field)
        return field * inverse, inverse

    def prepare_keys(head):
        if head < 2:
            loads["k", head].wait()
        normed, _ = key_normed(head)
        band[head, 0, 0] = (normed * k_gain[...]).astype(BF16)
        loads["v", head].wait()

    def prepare_queries(kv_head):
        for group in range(GROUPS):
            normed, _ = query_normed(kv_head * GROUPS + group)
            q_scaled[kv_head, pl.ds(group * TOK, TOK)] = (normed * q_gain[...] * SCALE).astype(BF16)

    def grads_of(kv_head):
        heads = range(kv_head * GROUPS, (kv_head + 1) * GROUPS)
        return jnp.concatenate([g_raw[:, head_columns(head)] for head in heads], axis=0)

    def prepare_mask():
        for distance in range(BAND):
            loads["s", distance].wait()
        query_seg = seg_rows[0].astype(F32)
        key_at = lax.broadcasted_iota(jnp.int32, (TOK, TOK), 0)
        query_at = lax.broadcasted_iota(jnp.int32, (TOK, TOK), 1)
        for distance in range(BAND):
            key_seg = jnp.where(me >= distance, seg_rows[distance].astype(F32), -1.0)
            key_column = jnp.broadcast_to(key_seg, (TOK, TOK)).T
            live = key_column == query_seg
            if distance == 0:
                live = live & (key_at <= query_at)
            if distance == GREACH:
                live = live & (key_at > query_at)
            weight = jnp.where(live, 1.0, 0.0)
            for group in range(GROUPS):
                mask[distance, :, pl.ds(group * TOK, TOK)] = weight

    stores = []

    def store(slot, source, target):
        copy = pltpu.make_async_copy(source, target, store_sem.at[slot])
        copy.start()
        stores.append(copy)

    def score(head, distances, state):
        total, weighted, weights, dprobs = state
        queries = q_scaled[head]
        grads = grads_of(head)
        for distance in distances:
            weight = jnp.exp(dot_nt(band[head, distance, 0], queries)) * mask[distance]
            dprob = dot_nt(band[head, distance, 1], grads)
            total = total + jnp.sum(weight, 0, keepdims=True)
            weighted = weighted + jnp.sum(weight * dprob, 0, keepdims=True)
            weights = weights | {distance: weight}
            dprobs = dprobs | {distance: dprob}
        return total, weighted, weights, dprobs

    def begin(head):
        band_copy(head, NEAR).wait_recv()
        zero = jnp.zeros((1, ROWS), F32)
        return score(head, (0, 2, 1), (zero, zero, {}, {}))

    def attend(head, state, after_gains=None):
        state = score(head, (4,), state)
        band_copy(head, FAR).wait_recv()
        total, weighted, weights, dprobs = score(head, (3,), state)
        queries = q_scaled[head]
        grads = grads_of(head)
        inverse = 1.0 / total
        centre = weighted * inverse
        probs, dscores = {}, {}
        dq_scaled = jnp.zeros((ROWS, HEAD_DIM), F32)
        for distance in range(BAND):
            prob = weights[distance] * inverse
            dscores[distance] = (prob * (dprobs[distance] - centre)).astype(BF16)
            probs[distance] = prob.astype(BF16)
            dq_scaled = dq_scaled + dot_tn(dscores[distance], band[head, distance, 0])
        key_gain_part = jnp.sum(dq_scaled * queries.astype(F32), 0, keepdims=True)
        query_gain_part = jnp.zeros((1, HEAD_DIM), F32)
        for group in range(GROUPS):
            normed, _ = query_normed(head * GROUPS + group)
            upstream = dq_scaled[group * TOK : (group + 1) * TOK] * SCALE
            query_gain_part = query_gain_part + jnp.sum(upstream * normed, 0, keepdims=True)
        both = jnp.concatenate([query_gain_part, key_gain_part], axis=0)
        gain_part[...] = both if head == 0 else gain_part[...] + both
        later = after_gains() if after_gains else None
        for distance in (1, 3):
            key_part = dot_nn(dscores[distance], queries)
            value_part = dot_nn(probs[distance], grads)
            part_out[head, distance // 2, 0] = key_part.astype(BF16)
            part_out[head, distance // 2, 1] = value_part.astype(BF16)
        attended = jnp.zeros((ROWS, HEAD_DIM), F32)
        for distance in (4, 2, 0):
            kept[head, distance // 2, 0] = dot_nn(dscores[distance], queries)
            kept[head, distance // 2, 1] = dot_nn(probs[distance], grads)
            if distance == 4:
                part_copy(head).start()
        for distance in range(BAND):
            attended = attended + dot_tn(probs[distance], band[head, distance, 1])
        for group in range(GROUPS):
            query_head = head * GROUPS + group
            rows = slice(group * TOK, (group + 1) * TOK)
            columns = head_columns(query_head)
            att_buf[:, columns] = attended[rows].astype(BF16)
            normed, inverse_q = query_normed(query_head)
            dq = norm_backward(dq_scaled[rows] * SCALE, normed, inverse_q, q_gain[...])
            dq_buf[:, columns] = dq.astype(BF16)
        return later

    def send_own(head):
        band_copy(head, NEXT).start()

    def pass_on(head):
        band_copy(head, NEXT).wait_recv()
        if head == 0:
            band_copy(head, FIRST).wait_recv()
        band_copy(head, RELAY).start()
        band_copy(head, NEAR).start()

    def share(head):
        band_copy(head, RELAY).wait_recv()
        band_copy(head, FAR).start()

    def join_parts(head):
        part_copy(head).wait_recv()
        kept[head, core] = kept[head, core] + part_in[head, 0].astype(F32)
        kept[head, core + 1] = kept[head, core + 1] + part_in[head, 1].astype(F32)
        sum_out[head, 0] = kept[head, 2].astype(BF16)
        sum_copy(head, 0).start()

    def pass_back(head):
        sum_copy(head, 0).wait_recv()
        sum_out[head, 1] = (kept[head, 1] + sum_in[head, 0].astype(F32)).astype(BF16)
        sum_copy(head, 1).start()

    def finish_keys(head):
        sum_copy(head, 1).wait_recv()
        dk = kept[head, 0, 0] + sum_in[head, 1, 0].astype(F32)
        dv = kept[head, 0, 1] + sum_in[head, 1, 1].astype(F32)
        columns = head_columns(head)
        dv_buf[:, columns] = dv.astype(BF16)
        normed, inverse = key_normed(head)
        dk = norm_backward(dk, normed, inverse, k_gain[...])
        dk_buf[:, columns] = dk.astype(BF16)

    def ar_copy(stage, source, target, device):
        return remote(source, target, ar_send.at[stage], ar_recv.at[stage], device)

    def ar_finish(stage, buffer, count):
        arrived = buffer.at[pl.ds(0, count)]
        copy = ar_copy(stage, arrived, arrived, partner)
        copy.wait_recv()
        copy.wait_send()

    def distance_of(step, size):
        return min(step, size - step)

    def sum_plane_start():
        gain_rows[0] = gain_part[0:1]
        gain_rows[1] = gain_part[1:2]
        slot = core * SIDE * SIDE + dp
        ar_plane[slot] = jnp.where(core == 0, gain_part[0:1], gain_part[1:2])
        steps = [(dy, dx) for dy in range(SIDE) for dx in range(SIDE)]
        for dy, dx in sorted(steps, key=lambda step: -sum(distance_of(each, SIDE) for each in step)):
            other = wrap(y + dy, SIDE) * SIDE + wrap(x + dx, SIDE)
            ar_copy(0, gain_rows.at[1 - core], ar_plane.at[slot], (other, partner[1])).start()
            if (dy, dx) != (0, 0):
                ar_copy(0, gain_rows.at[core], ar_plane.at[slot], (other, me)).start()

    def sum_z_start():
        ar_finish(0, ar_plane, 2 * SIDE * SIDE - 1)
        ar_z[z] = jnp.sum(ar_plane[...], 0)
        for step in sorted(range(1, chips), key=lambda step: -distance_of(step, chips)):
            other = wrap(z + step, chips)
            ar_copy(1, ar_z.at[z], ar_z.at[z], (dp, other * 2 + core)).start()

    def share_rows():
        ar_finish(1, ar_z, chips - 1)
        ar_core[core] = jnp.sum(ar_z[...], 0)
        ar_copy(2, ar_core.at[core], ar_core.at[core], partner).start()
        ar_finish(2, ar_core, 1)

    pl.semaphore_wait(barrier, len(nearby) + 1)
    band_copy(0, FIRST).start()
    loads["k_gain"].wait()
    prepare_keys(0)
    send_own(0)
    tell(0, nearby)
    prepare_keys(1)
    send_own(1)
    prepare_keys(2)
    prepare_keys(3)
    loads["q_gain"].wait()
    loads["q"].wait()
    prepare_queries(0)
    hear(0, len(nearby))
    tell(1, [along_z(2), along_z(-2), along_x(2), along_y(2)])
    prepare_mask()
    pass_on(0)
    send_own(2)
    prepare_queries(1)
    hear(1, 4)
    tell(2, [along_z(4), along_z(-4), partner])
    pass_on(1)
    send_own(3)
    prepare_queries(2)
    prepare_queries(3)
    loads["g"].wait()
    state = begin(0)
    share(0)
    attend(0, state)
    pass_on(2)
    hear(2, 3)
    tell(3, [along_z(8), along_z(-8)])
    join_parts(0)
    state = begin(1)
    share(1)
    attend(1, state)
    pass_on(3)
    join_parts(1)
    pass_back(0)
    state = begin(2)
    share(2)
    attend(2, state)
    hear(3, 2)
    state = begin(3)
    share(3)
    attend(3, state, sum_plane_start)
    store(0, att_buf, att_hbm.at[0])
    store(1, dq_buf, dq_hbm.at[0])
    join_parts(2)
    pass_back(1)
    finish_keys(0)
    join_parts(3)
    sum_z_start()
    pass_back(2)
    finish_keys(1)
    pass_back(3)
    finish_keys(2)
    early = pl.ds(0, (KV_HEADS - 1) * HEAD_DIM)
    last = head_columns(KV_HEADS - 1)
    store(2, dk_buf.at[:, early], dk_hbm.at[0, :, early])
    store(3, dv_buf.at[:, early], dv_hbm.at[0, :, early])
    finish_keys(3)
    store(4, dk_buf.at[:, last], dk_hbm.at[0, :, last])
    store(5, dv_buf.at[:, last], dv_hbm.at[0, :, last])
    share_rows()
    gain_grads[0] = ar_core[0] * factor
    gain_grads[1] = ar_core[1] * factor / k_gain[...]
    store(6, gain_grads.at[0], q_gain_grad_hbm)
    store(7, gain_grads.at[1], k_gain_grad_hbm)

    sent = band.at[:, pl.ds(0, 4)]
    remote(sent, sent, band_send, band_recv.at[0, 0], ahead).wait_send()
    remote(part_out, part_out, part_send, part_recv.at[0], partner).wait_send()
    remote(sum_out, sum_out, sum_send, sum_recv.at[0, 0], behind).wait_send()
    for copy in stores:
        copy.wait()


def hand_over(count, *refs):
    sources, targets = refs[:count], refs[count : 2 * count]
    buffers, semaphores = refs[2 * count : 3 * count], refs[3 * count]
    loads = [
        pltpu.make_async_copy(source, buffer, semaphores.at[0, slot])
        for slot, (source, buffer) in enumerate(zip(sources, buffers))
    ]
    stores = [
        pltpu.make_async_copy(buffer, target, semaphores.at[1, slot])
        for slot, (buffer, target) in enumerate(zip(buffers, targets))
    ]
    for load in loads:
        load.start()
    for load, store in zip(loads, stores):
        load.wait()
        store.start()
    for store in stores:
        store.wait()


def shards(segment_ids, queries, keys, values, query_gain, key_gain, out_grad):
    ctx_size = lax.axis_size("ctx")
    factor = (lax.axis_size("dp") * queries.shape[0] * ctx_size * queries.shape[1]) ** (-0.5)
    width = KV_HEADS * HEAD_DIM
    hbm = pl.BlockSpec(memory_space=pl.ANY)
    dma = pltpu.SemaphoreType.DMA
    pair = (2, TOK, HEAD_DIM)
    chips = ctx_size // 2
    shapes = (
        jax.ShapeDtypeStruct((1, TOK, HEADS * HEAD_DIM), BF16),
        jax.ShapeDtypeStruct((1, TOK, HEADS * HEAD_DIM), BF16),
        jax.ShapeDtypeStruct((1, TOK, width), BF16),
        jax.ShapeDtypeStruct((1, TOK, width), BF16),
        jax.ShapeDtypeStruct((1, HEAD_DIM), F32),
        jax.ShapeDtypeStruct((1, HEAD_DIM), F32),
    )
    outs = pl.pallas_call(
        lambda *refs: kernel(ctx_size, factor, *refs),
        out_shape=shapes,
        in_specs=[hbm] * 7,
        out_specs=(hbm,) * len(shapes),
        scratch_shapes=[
            pltpu.VMEM((1, HEAD_DIM), F32),
            pltpu.VMEM((1, HEAD_DIM), F32),
            pltpu.VMEM((BAND, 1, TOK), jnp.int32),
            pltpu.VMEM((BAND, TOK, ROWS), F32),
            pltpu.VMEM((TOK, HEADS * HEAD_DIM), BF16),
            pltpu.VMEM((KV_HEADS, ROWS, HEAD_DIM), BF16),
            pltpu.VMEM((TOK, HEADS * HEAD_DIM), BF16),
            pltpu.VMEM((TOK, width), BF16),
            pltpu.VMEM((KV_HEADS, BAND) + pair, BF16),
            pltpu.VMEM((KV_HEADS, 2) + pair, BF16),
            pltpu.VMEM((KV_HEADS, 2) + pair, BF16),
            pltpu.VMEM((KV_HEADS, 3) + pair, F32),
            pltpu.VMEM((KV_HEADS, 2) + pair, BF16),
            pltpu.VMEM((KV_HEADS, 2) + pair, BF16),
            pltpu.VMEM((TOK, HEADS * HEAD_DIM), BF16),
            pltpu.VMEM((TOK, HEADS * HEAD_DIM), BF16),
            pltpu.VMEM((TOK, width), BF16),
            pltpu.VMEM((TOK, width), BF16),
            pltpu.VMEM((2, HEAD_DIM), F32),
            pltpu.VMEM((2, 1, HEAD_DIM), F32),
            pltpu.VMEM((2, 1, HEAD_DIM), F32),
            pltpu.VMEM((2 * SIDE * SIDE, 1, HEAD_DIM), F32),
            pltpu.VMEM((chips, 1, HEAD_DIM), F32),
            pltpu.VMEM((2, 1, HEAD_DIM), F32),
            dma((10 + BAND,)),
            dma((8,)),
            dma,
            dma((KV_HEADS, 5)),
            dma,
            dma((KV_HEADS,)),
            dma,
            dma((KV_HEADS, 2)),
            dma((3,)),
            dma((3,)),
            pltpu.SemaphoreType.REGULAR((4,)),
        ],
        compiler_params=pltpu.CompilerParams(
            collective_id=0, has_side_effects=True, vmem_limit_bytes=67043328
        ),
    )(
        segment_ids,
        queries,
        keys,
        values,
        query_gain.reshape(1, HEAD_DIM),
        key_gain.reshape(1, HEAD_DIM),
        out_grad,
    )
    outs = pl.pallas_call(
        lambda *refs: hand_over(len(shapes), *refs),
        out_shape=shapes,
        in_specs=[hbm] * len(shapes),
        out_specs=(hbm,) * len(shapes),
        scratch_shapes=[pltpu.VMEM(shape.shape, shape.dtype) for shape in shapes]
        + [dma((2, len(shapes)))],
        compiler_params=pltpu.CompilerParams(vmem_limit_bytes=67043328),
    )(*outs)
    return (*outs[:4], outs[4].reshape(HEAD_DIM), outs[5].reshape(HEAD_DIM))


def solution(mesh):
    blocks = P("dp", "ctx", None)
    return jax.shard_map(
        shards,
        mesh=mesh,
        in_specs=(P("dp", None), blocks, blocks, blocks, P(), P(), blocks),
        out_specs=(blocks, blocks, blocks, blocks, P(), P()),
        check_vma=False,
    )
```

```python
import jax
import jax.numpy as jnp
from jax import lax
from jax.experimental import pallas as pl
from jax.experimental.pallas import tpu as pltpu
from jax.sharding import PartitionSpec as P

HEADS = 8
KV_HEADS = 4
GROUPS = HEADS // KV_HEADS
HEAD_DIM = 256
TOK = 128
GREACH = 4
BAND = GREACH + 1
ROWS = GROUPS * TOK
SIDE = 4
EPSILON = 1e-06
SCALE = HEAD_DIM ** (-0.5)

MESH = pl.DeviceIdType.MESH
F32 = jnp.float32
BF16 = jnp.bfloat16

NEXT, RELAY, NEAR, FAR, FIRST = range(5)


def wrap(value, size):
    return lax.rem(value + size, size)


def dot_nt(a, b):
    return lax.dot_general(a, b, (((1,), (1,)), ((), ())), preferred_element_type=F32)


def dot_tn(a, b):
    return lax.dot_general(a, b, (((0,), (0,)), ((), ())), preferred_element_type=F32)


def dot_nn(a, b):
    return lax.dot_general(a, b, (((1,), (0,)), ((), ())), preferred_element_type=F32)


def inverse_norm(field):
    return lax.rsqrt(jnp.mean(field * field, -1, keepdims=True) + EPSILON)


def norm_backward(upstream, normed, inverse, gain):
    scaled = upstream * gain
    return inverse * (scaled - normed * jnp.mean(scaled * normed, -1, keepdims=True))


def head_columns(head):
    return pl.ds(head * HEAD_DIM, HEAD_DIM)


def kernel(
    ctx_size,
    factor,
    seg_hbm,
    q_hbm,
    k_hbm,
    v_hbm,
    q_gain_hbm,
    k_gain_hbm,
    g_hbm,
    att_hbm,
    dq_hbm,
    dk_hbm,
    dv_hbm,
    q_gain_grad_hbm,
    k_gain_grad_hbm,
    q_gain,
    k_gain,
    seg_rows,
    mask,
    q_raw,
    q_scaled,
    g_raw,
    k_raw,
    band,
    part_out,
    part_in,
    kept,
    sum_out,
    sum_in,
    att_buf,
    dq_buf,
    dk_buf,
    dv_buf,
    gain_part,
    gain_rows,
    gain_grads,
    ar_plane,
    ar_z,
    ar_core,
    load_sem,
    store_sem,
    band_send,
    band_recv,
    part_send,
    part_recv,
    sum_send,
    sum_recv,
    ar_send,
    ar_recv,
    known,
):
    dp = lax.axis_index("dp")
    me = lax.axis_index("ctx")
    core = lax.rem(me, 2)
    z = lax.div(me, 2)
    x = lax.rem(dp, SIDE)
    y = lax.div(dp, SIDE)
    chips = ctx_size // 2

    partner = (dp, me + 1 - 2 * core)

    def along_z(step):
        return (dp, wrap(me + 2 * step, ctx_size))

    def along_x(step):
        return (y * SIDE + wrap(x + step, SIDE), me)

    def along_y(step):
        return (wrap(y + step, SIDE) * SIDE + x, me)

    ahead = along_z(1)
    behind = along_z(-1)

    nearby = [along_z(1), along_z(-1), along_x(1), along_x(-1), along_y(1), along_y(-1)]
    barrier = pltpu.get_barrier_semaphore()
    for device in nearby + [partner]:
        pl.semaphore_signal(barrier, inc=1, device_id=device, device_id_type=MESH)

    loads = {}

    def load(name, slot, source, target):
        copy = pltpu.make_async_copy(source, target, load_sem.at[slot])
        copy.start()
        loads[name] = copy

    rest = pl.ds(HEAD_DIM, (KV_HEADS - 1) * HEAD_DIM)
    load("k_gain", 0, k_gain_hbm, k_gain)
    load(("k", 0), 1, k_hbm.at[0, :, head_columns(0)], k_raw.at[:, head_columns(0)])
    load(("v", 0), 2, v_hbm.at[0, :, head_columns(0)], band.at[0, 0, 1])
    load(("k", 1), 3, k_hbm.at[0, :, rest], k_raw.at[:, rest])
    for head in range(1, KV_HEADS):
        load(("v", head), 3 + head, v_hbm.at[0, :, head_columns(head)], band.at[head, 0, 1])
    load("q_gain", 7, q_gain_hbm, q_gain)
    load("q", 8, q_hbm.at[0], q_raw)
    load("g", 9, g_hbm.at[0], g_raw)
    for distance in range(BAND):
        first = pl.multiple_of(jnp.maximum(me - distance, 0) * TOK, TOK)
        load(("s", distance), 10 + distance, seg_hbm.at[:, pl.ds(first, TOK)], seg_rows.at[distance])

    def remote(source, target, send, recv, device):
        return pltpu.make_async_remote_copy(
            src_ref=source,
            dst_ref=target,
            send_sem=send,
            recv_sem=recv,
            device_id=device,
            device_id_type=MESH,
        )

    def band_copy(head, kind):
        slot, target, device = {
            NEXT: (0, 2, ahead),
            RELAY: (2, 4, ahead),
            NEAR: (2 * core, 1, partner),
            FAR: (2 + 2 * core, 3, partner),
            FIRST: (0, 2, ahead),
        }[kind]
        source, target = band.at[head, slot], band.at[head, target]
        if kind == FIRST:
            source, target = v_hbm.at[0, :, head_columns(head)], band.at[head, 2, 1]
        elif kind == NEXT and head == 0:
            source, target = band.at[head, 0, 0], band.at[head, 2, 0]
        return remote(
            source,
            target,
            band_send,
            band_recv.at[head, kind],
            device,
        )

    def part_copy(head):
        return remote(
            part_out.at[head], part_in.at[head], part_send, part_recv.at[head], partner
        )

    def sum_copy(head, stage):
        return remote(
            sum_out.at[head, stage],
            sum_in.at[head, stage],
            sum_send,
            sum_recv.at[head, stage],
            behind,
        )

    def tell(stage, devices):
        for device in devices:
            pl.semaphore_signal(known.at[stage], inc=1, device_id=device, device_id_type=MESH)

    def hear(stage, count):
        pl.semaphore_wait(known.at[stage], count)

    def key_normed(head):
        field = k_raw[:, head_columns(head)].astype(F32)
        inverse = inverse_norm(field)
        return field * inverse, inverse

    def query_normed(head):
        field = q_raw[:, head_columns(head)].astype(F32)
        inverse = inverse_norm(field)
        return field * inverse, inverse

    def prepare_keys(head):
        if head < 2:
            loads["k", head].wait()
        normed, _ = key_normed(head)
        band[head, 0, 0] = (normed * k_gain[...]).astype(BF16)
        loads["v", head].wait()

    def prepare_queries(kv_head):
        for group in range(GROUPS):
            normed, _ = query_normed(kv_head * GROUPS + group)
            q_scaled[kv_head, pl.ds(group * TOK, TOK)] = (normed * q_gain[...] * SCALE).astype(BF16)

    def grads_of(kv_head):
        heads = range(kv_head * GROUPS, (kv_head + 1) * GROUPS)
        return jnp.concatenate([g_raw[:, head_columns(head)] for head in heads], axis=0)

    def prepare_mask():
        for distance in range(BAND):
            loads["s", distance].wait()
        query_seg = seg_rows[0].astype(F32)
        key_at = lax.broadcasted_iota(jnp.int32, (TOK, TOK), 0)
        query_at = lax.broadcasted_iota(jnp.int32, (TOK, TOK), 1)
        for distance in range(BAND):
            key_seg = jnp.where(me >= distance, seg_rows[distance].astype(F32), -1.0)
            key_column = jnp.broadcast_to(key_seg, (TOK, TOK)).T
            live = key_column == query_seg
            if distance == 0:
                live = live & (key_at <= query_at)
            if distance == GREACH:
                live = live & (key_at > query_at)
            weight = jnp.where(live, 1.0, 0.0)
            for group in range(GROUPS):
                mask[distance, :, pl.ds(group * TOK, TOK)] = weight

    stores = []

    def store(slot, source, target):
        copy = pltpu.make_async_copy(source, target, store_sem.at[slot])
        copy.start()
        stores.append(copy)

    def score(head, distances, state):
        total, weighted, weights, dprobs = state
        queries = q_scaled[head]
        grads = grads_of(head)
        for distance in distances:
            weight = jnp.exp(dot_nt(band[head, distance, 0], queries)) * mask[distance]
            dprob = dot_nt(band[head, distance, 1], grads)
            total = total + jnp.sum(weight, 0, keepdims=True)
            weighted = weighted + jnp.sum(weight * dprob, 0, keepdims=True)
            weights = weights | {distance: weight}
            dprobs = dprobs | {distance: dprob}
        return total, weighted, weights, dprobs

    def begin(head):
        band_copy(head, NEAR).wait_recv()
        zero = jnp.zeros((1, ROWS), F32)
        return score(head, (0, 2, 1), (zero, zero, {}, {}))

    def attend(head, state, after_gains=None):
        state = score(head, (4,), state)
        band_copy(head, FAR).wait_recv()
        total, weighted, weights, dprobs = score(head, (3,), state)
        queries = q_scaled[head]
        grads = grads_of(head)
        inverse = 1.0 / total
        centre = weighted * inverse
        probs, dscores = {}, {}
        dq_scaled = jnp.zeros((ROWS, HEAD_DIM), F32)
        for distance in range(BAND):
            prob = weights[distance] * inverse
            dscores[distance] = (prob * (dprobs[distance] - centre)).astype(BF16)
            probs[distance] = prob.astype(BF16)
            dq_scaled = dq_scaled + dot_tn(dscores[distance], band[head, distance, 0])
        key_gain_part = jnp.sum(dq_scaled * queries.astype(F32), 0, keepdims=True)
        query_gain_part = jnp.zeros((1, HEAD_DIM), F32)
        for group in range(GROUPS):
            normed, _ = query_normed(head * GROUPS + group)
            upstream = dq_scaled[group * TOK : (group + 1) * TOK] * SCALE
            query_gain_part = query_gain_part + jnp.sum(upstream * normed, 0, keepdims=True)
        both = jnp.concatenate([query_gain_part, key_gain_part], axis=0)
        gain_part[...] = both if head == 0 else gain_part[...] + both
        later = after_gains() if after_gains else None
        for distance in (1, 3):
            key_part = dot_nn(dscores[distance], queries)
            value_part = dot_nn(probs[distance], grads)
            part_out[head, distance // 2, 0] = key_part.astype(BF16)
            part_out[head, distance // 2, 1] = value_part.astype(BF16)
        attended = jnp.zeros((ROWS, HEAD_DIM), F32)
        for distance in (4, 2, 0):
            kept[head, distance // 2, 0] = dot_nn(dscores[distance], queries)
            kept[head, distance // 2, 1] = dot_nn(probs[distance], grads)
            if distance == 4:
                part_copy(head).start()
        for distance in range(BAND):
            attended = attended + dot_tn(probs[distance], band[head, distance, 1])
        for group in range(GROUPS):
            query_head = head * GROUPS + group
            rows = slice(group * TOK, (group + 1) * TOK)
            columns = head_columns(query_head)
            att_buf[:, columns] = attended[rows].astype(BF16)
            normed, inverse_q = query_normed(query_head)
            dq = norm_backward(dq_scaled[rows] * SCALE, normed, inverse_q, q_gain[...])
            dq_buf[:, columns] = dq.astype(BF16)
        return later

    def send_own(head):
        band_copy(head, NEXT).start()

    def pass_on(head):
        band_copy(head, NEXT).wait_recv()
        if head == 0:
            band_copy(head, FIRST).wait_recv()
        band_copy(head, RELAY).start()
        band_copy(head, NEAR).start()

        @pl.when(core == 0)
        def _():
            band_copy(head, FAR).start()

    def share(head):
        band_copy(head, RELAY).wait_recv()

        @pl.when(core == 1)
        def _():
            band_copy(head, FAR).start()

    def join_parts(head):
        part_copy(head).wait_recv()
        kept[head, core] = kept[head, core] + part_in[head, 0].astype(F32)
        kept[head, core + 1] = kept[head, core + 1] + part_in[head, 1].astype(F32)
        sum_out[head, 0] = kept[head, 2].astype(BF16)
        sum_copy(head, 0).start()

    def pass_back(head):
        sum_copy(head, 0).wait_recv()
        sum_out[head, 1] = (kept[head, 1] + sum_in[head, 0].astype(F32)).astype(BF16)
        sum_copy(head, 1).start()

    def finish_keys(head):
        sum_copy(head, 1).wait_recv()
        dk = kept[head, 0, 0] + sum_in[head, 1, 0].astype(F32)
        dv = kept[head, 0, 1] + sum_in[head, 1, 1].astype(F32)
        columns = head_columns(head)
        dv_buf[:, columns] = dv.astype(BF16)
        normed, inverse = key_normed(head)
        dk = norm_backward(dk, normed, inverse, k_gain[...])
        dk_buf[:, columns] = dk.astype(BF16)

    def ar_copy(stage, source, target, device):
        return remote(source, target, ar_send.at[stage], ar_recv.at[stage], device)

    def ar_finish(stage, buffer, count):
        arrived = buffer.at[pl.ds(0, count)]
        copy = ar_copy(stage, arrived, arrived, partner)
        copy.wait_recv()
        copy.wait_send()

    def distance_of(step, size):
        return min(step, size - step)

    def sum_plane_start():
        gain_rows[0] = gain_part[0:1]
        gain_rows[1] = gain_part[1:2]
        slot = core * SIDE * SIDE + dp
        ar_plane[slot] = jnp.where(core == 0, gain_part[0:1], gain_part[1:2])
        steps = [(dy, dx) for dy in range(SIDE) for dx in range(SIDE)]
        for dy, dx in sorted(steps, key=lambda step: -sum(distance_of(each, SIDE) for each in step)):
            other = wrap(y + dy, SIDE) * SIDE + wrap(x + dx, SIDE)
            ar_copy(0, gain_rows.at[1 - core], ar_plane.at[slot], (other, partner[1])).start()
            if (dy, dx) != (0, 0):
                ar_copy(0, gain_rows.at[core], ar_plane.at[slot], (other, me)).start()

    def sum_z_start():
        ar_finish(0, ar_plane, 2 * SIDE * SIDE - 1)
        ar_z[z] = jnp.sum(ar_plane[...], 0)
        for step in sorted(range(1, chips), key=lambda step: -distance_of(step, chips)):
            other = wrap(z + step, chips)
            ar_copy(1, ar_z.at[z], ar_z.at[z], (dp, other * 2 + core)).start()

    def share_rows():
        ar_finish(1, ar_z, chips - 1)
        ar_core[core] = jnp.sum(ar_z[...], 0)
        ar_copy(2, ar_core.at[core], ar_core.at[core], partner).start()
        ar_finish(2, ar_core, 1)

    pl.semaphore_wait(barrier, len(nearby) + 1)
    band_copy(0, FIRST).start()
    loads["k_gain"].wait()
    prepare_keys(0)
    send_own(0)
    tell(0, nearby)
    prepare_keys(1)
    send_own(1)
    prepare_keys(2)
    prepare_keys(3)
    loads["q_gain"].wait()
    loads["q"].wait()
    prepare_queries(0)
    hear(0, len(nearby))
    tell(1, [along_z(2), along_z(-2), along_x(2), along_y(2)])
    prepare_mask()
    pass_on(0)
    send_own(2)
    prepare_queries(1)
    hear(1, 4)
    tell(2, [along_z(4), along_z(-4), partner])
    pass_on(1)
    send_own(3)
    prepare_queries(2)
    prepare_queries(3)
    loads["g"].wait()
    state = begin(0)
    share(0)
    attend(0, state)
    pass_on(2)
    hear(2, 3)
    tell(3, [along_z(8), along_z(-8)])
    join_parts(0)
    state = begin(1)
    share(1)
    attend(1, state)
    pass_on(3)
    join_parts(1)
    pass_back(0)
    state = begin(2)
    share(2)
    attend(2, state)
    hear(3, 2)
    state = begin(3)
    share(3)
    join_parts(2)
    pass_back(1)
    attend(3, state, sum_plane_start)
    store(0, att_buf, att_hbm.at[0])
    store(1, dq_buf, dq_hbm.at[0])
    finish_keys(0)
    join_parts(3)
    sum_z_start()
    pass_back(2)
    finish_keys(1)
    pass_back(3)
    finish_keys(2)
    early = pl.ds(0, (KV_HEADS - 1) * HEAD_DIM)
    last = head_columns(KV_HEADS - 1)
    store(2, dk_buf.at[:, early], dk_hbm.at[0, :, early])
    store(3, dv_buf.at[:, early], dv_hbm.at[0, :, early])
    finish_keys(3)
    store(4, dk_buf.at[:, last], dk_hbm.at[0, :, last])
    store(5, dv_buf.at[:, last], dv_hbm.at[0, :, last])
    share_rows()
    gain_grads[0] = ar_core[0] * factor
    gain_grads[1] = ar_core[1] * factor / k_gain[...]
    store(6, gain_grads.at[0], q_gain_grad_hbm)
    store(7, gain_grads.at[1], k_gain_grad_hbm)

    sent = band.at[:, pl.ds(0, 4)]
    remote(sent, sent, band_send, band_recv.at[0, 0], ahead).wait_send()
    remote(part_out, part_out, part_send, part_recv.at[0], partner).wait_send()
    remote(sum_out, sum_out, sum_send, sum_recv.at[0, 0], behind).wait_send()
    for copy in stores:
        copy.wait()


def hand_over(count, *refs):
    sources, targets = refs[:count], refs[count : 2 * count]
    buffers, semaphores = refs[2 * count : 3 * count], refs[3 * count]
    loads = [
        pltpu.make_async_copy(source, buffer, semaphores.at[0, slot])
        for slot, (source, buffer) in enumerate(zip(sources, buffers))
    ]
    stores = [
        pltpu.make_async_copy(buffer, target, semaphores.at[1, slot])
        for slot, (buffer, target) in enumerate(zip(buffers, targets))
    ]
    for load in loads:
        load.start()
    for load, store in zip(loads, stores):
        load.wait()
        store.start()
    for store in stores:
        store.wait()


def shards(segment_ids, queries, keys, values, query_gain, key_gain, out_grad):
    ctx_size = lax.axis_size("ctx")
    factor = (lax.axis_size("dp") * queries.shape[0] * ctx_size * queries.shape[1]) ** (-0.5)
    width = KV_HEADS * HEAD_DIM
    hbm = pl.BlockSpec(memory_space=pl.ANY)
    dma = pltpu.SemaphoreType.DMA
    pair = (2, TOK, HEAD_DIM)
    chips = ctx_size // 2
    shapes = (
        jax.ShapeDtypeStruct((1, TOK, HEADS * HEAD_DIM), BF16),
        jax.ShapeDtypeStruct((1, TOK, HEADS * HEAD_DIM), BF16),
        jax.ShapeDtypeStruct((1, TOK, width), BF16),
        jax.ShapeDtypeStruct((1, TOK, width), BF16),
        jax.ShapeDtypeStruct((1, HEAD_DIM), F32),
        jax.ShapeDtypeStruct((1, HEAD_DIM), F32),
    )
    outs = pl.pallas_call(
        lambda *refs: kernel(ctx_size, factor, *refs),
        out_shape=shapes,
        in_specs=[hbm] * 7,
        out_specs=(hbm,) * len(shapes),
        scratch_shapes=[
            pltpu.VMEM((1, HEAD_DIM), F32),
            pltpu.VMEM((1, HEAD_DIM), F32),
            pltpu.VMEM((BAND, 1, TOK), jnp.int32),
            pltpu.VMEM((BAND, TOK, ROWS), F32),
            pltpu.VMEM((TOK, HEADS * HEAD_DIM), BF16),
            pltpu.VMEM((KV_HEADS, ROWS, HEAD_DIM), BF16),
            pltpu.VMEM((TOK, HEADS * HEAD_DIM), BF16),
            pltpu.VMEM((TOK, width), BF16),
            pltpu.VMEM((KV_HEADS, BAND) + pair, BF16),
            pltpu.VMEM((KV_HEADS, 2) + pair, BF16),
            pltpu.VMEM((KV_HEADS, 2) + pair, BF16),
            pltpu.VMEM((KV_HEADS, 3) + pair, F32),
            pltpu.VMEM((KV_HEADS, 2) + pair, BF16),
            pltpu.VMEM((KV_HEADS, 2) + pair, BF16),
            pltpu.VMEM((TOK, HEADS * HEAD_DIM), BF16),
            pltpu.VMEM((TOK, HEADS * HEAD_DIM), BF16),
            pltpu.VMEM((TOK, width), BF16),
            pltpu.VMEM((TOK, width), BF16),
            pltpu.VMEM((2, HEAD_DIM), F32),
            pltpu.VMEM((2, 1, HEAD_DIM), F32),
            pltpu.VMEM((2, 1, HEAD_DIM), F32),
            pltpu.VMEM((2 * SIDE * SIDE, 1, HEAD_DIM), F32),
            pltpu.VMEM((chips, 1, HEAD_DIM), F32),
            pltpu.VMEM((2, 1, HEAD_DIM), F32),
            dma((10 + BAND,)),
            dma((8,)),
            dma,
            dma((KV_HEADS, 5)),
            dma,
            dma((KV_HEADS,)),
            dma,
            dma((KV_HEADS, 2)),
            dma((3,)),
            dma((3,)),
            pltpu.SemaphoreType.REGULAR((4,)),
        ],
        compiler_params=pltpu.CompilerParams(
            collective_id=0, has_side_effects=True, vmem_limit_bytes=67043328
        ),
    )(
        segment_ids,
        queries,
        keys,
        values,
        query_gain.reshape(1, HEAD_DIM),
        key_gain.reshape(1, HEAD_DIM),
        out_grad,
    )
    outs = pl.pallas_call(
        lambda *refs: hand_over(len(shapes), *refs),
        out_shape=shapes,
        in_specs=[hbm] * len(shapes),
        out_specs=(hbm,) * len(shapes),
        scratch_shapes=[pltpu.VMEM(shape.shape, shape.dtype) for shape in shapes]
        + [dma((2, len(shapes)))],
        compiler_params=pltpu.CompilerParams(vmem_limit_bytes=67043328),
    )(*outs)
    return (*outs[:4], outs[4].reshape(HEAD_DIM), outs[5].reshape(HEAD_DIM))


def solution(mesh):
    blocks = P("dp", "ctx", None)
    return jax.shard_map(
        shards,
        mesh=mesh,
        in_specs=(P("dp", None), blocks, blocks, blocks, P(), P(), blocks),
        out_specs=(blocks, blocks, blocks, blocks, P(), P()),
        check_vma=False,
    )
```
